32 devices in a mesh: elem: 8 (over z, core), front: 4 (over y, x).
Axes of the slice: x: 2, y: 2, z: 4, core: 2. Of those that a mesh axis runs over, the one named last changes fastest.
Arguments:
- elem_mat: bfloat16 [24, 24, 4096], P(None, None, ('elem', 'front')), may hold values from -1.25 to 1.25
- elem_deriv: bfloat16 [24, 24, 4096], P(None, None, ('elem', 'front')), may hold values from -1.1953125 to 1.1953125
- elem_disp: bfloat16 [24, 4096], P(None, ('elem', 'front')), may hold values from -6 to 6
- elem_sens: bfloat16 [4096, 24, 512], P(('elem', 'front')), may hold values from -3 to 3
- design_var: int32 [4096], P(('elem', 'front')), may hold values from 0 to 511
- dof_rows: int32 [24, 4096], P(None, ('elem', 'front')), may hold values from 0 to 14336, as said below
- inverse_factor: bfloat16 [57344, 8192], P('front', 'elem'), may hold values from -2 to 2
- coupling: bfloat16 [8192, 49152], P('elem', 'front'), may hold values from -0.0625 to 0.0625
- front_sizes: int32 [7], replicated, may hold values from 4096 to 8192
Outputs:
- sens: float32 [57344, 512], P('front', 'elem')
The draws below stay inside these ranges and needn't reach their ends.
Inputs may be any that keep to these rules, and one draw needn't show every extreme that they name: `dof_rows`: the used rows of one element lie in one aligned block of 128 rows; the value 14336 marks a degree of freedom that no front holds.
All inputs are finite; a program needn't handle non-finite values.
Results may differ from the reference program's by a relative error of at most 0.014.
Values may be sent and summed in bfloat16 or wider, within the bound.
A program may use at most 128 MiB of HBM per device.

```python
import jax
import jax.numpy as jnp
from jax import lax

DOF = 24
NRHS = 512
FS = 8192
LEVELS = 3
BLK = 128
E_DEV = 128
ELEMS = 4096
LR = 14336
CR = 12288
FRONTS = 7
N_FRONT = 4


def draw_dof_rows(key, part):
    key_block = jax.random.fold_in(key, 11)
    key_offset = jax.random.fold_in(key, 12)
    key_unused = jax.random.fold_in(key, 13)
    block_index = jax.random.randint(key_block, (1, ELEMS), 0, LR // BLK)
    offsets = jax.random.randint(key_offset, (DOF, ELEMS), 0, BLK)
    unused = jax.random.randint(key_unused, (DOF, ELEMS), 0, 8)
    places = block_index * BLK + offsets
    return jnp.where(unused == 0, LR, places).astype(jnp.int32)


def draw_inverse_factor(key, part):
    total_rows = N_FRONT * LR
    row_at = jnp.arange(total_rows, dtype=jnp.int32)
    device_at = row_at // LR
    spot_at = row_at % LR
    global_row = jnp.zeros_like(row_at)
    start_spot = 0
    for level_at in range(LEVELS):
        share_count = N_FRONT >> LEVELS - 1 - level_at
        block_rows = FS // share_count
        inside = (spot_at >= start_spot) & (spot_at < start_spot + block_rows)
        global_row = jnp.where(inside, device_at % share_count * block_rows + spot_at - start_spot, global_row)
        start_spot = start_spot + block_rows
    key_off = jax.random.fold_in(key, 21)
    key_diag = jax.random.fold_in(key, 22)
    spread_part = jax.random.normal(key_off, (total_rows, FS), jnp.float32) * (0.5 / FS ** 0.5)
    diag_part = jax.random.uniform(key_diag, (total_rows,), jnp.float32, 0.6, 1.2)
    spread_part = jnp.clip(spread_part, -1.0, 1.0)
    columns_at = jnp.arange(FS, dtype=jnp.int32)
    on_diag = (columns_at[None, :] == global_row[:, None]).astype(jnp.float32)
    return (spread_part * (1.0 - on_diag) + on_diag * diag_part[:, None]).astype(jnp.bfloat16)


def place_ends(result, key, least, largest):
    spot = [jax.random.randint(jax.random.fold_in(key, axis), (), 0, length) for axis, length in enumerate(result.shape)]
    widest = result.shape.index(max(result.shape))
    next_to = spot[:widest] + [(spot[widest] + 1) % result.shape[widest]] + spot[widest + 1:]
    return result.at[tuple(spot)].set(least).at[tuple(next_to)].set(largest)


def block_scale(stream_key, dims, cuts, least, high):
    factor_of, own = 1.0, jax.random.fold_in(stream_key, 6)
    for position, blocks in cuts:
        draws = jnp.exp(jax.random.uniform(jax.random.fold_in(own, position), (blocks,), jnp.float32, least / len(cuts), high / len(cuts)))
        factor_of = factor_of * jnp.repeat(draws, dims[position] // blocks).reshape([-1 if axis == position else 1 for axis in range(len(dims))])
    return factor_of


def gaussian(rng, extent, scale, reach, shards=(), kind=jnp.bfloat16):
    entries = jax.random.normal(rng, extent, jnp.float32) * scale
    if len(shards) > 0:
        entries = block_scale(rng, extent, shards, -0.22, 0.18) * entries
    return jnp.clip(entries, min=-reach, max=reach).astype(kind)


def setup_inputs(seed: int = 0) -> dict:
    key_of = jax.random.split(jax.random.key(seed), 10)
    return {
        "elem_mat": gaussian(key_of[0], (DOF, DOF, ELEMS), DOF ** -0.5, 1.25, ((2, 32),)),
        "elem_deriv": gaussian(key_of[1], (DOF, DOF, ELEMS), 0.2, 1.1953125, ((2, 32),)),
        "elem_disp": gaussian(key_of[2], (DOF, ELEMS), 1.0, 6.0, ((1, 32),)),
        "elem_sens": gaussian(key_of[3], (ELEMS, DOF, NRHS), 0.5, 3.0, ((0, 32),)),
        "design_var": place_ends(jax.random.randint(key_of[4], (ELEMS,), 0, NRHS), jax.random.fold_in(key_of[4], 1), 0, NRHS - 1).astype(jnp.int32),
        "dof_rows": draw_dof_rows(jax.random.fold_in(key_of[9], 71), 0),
        "inverse_factor": draw_inverse_factor(jax.random.fold_in(key_of[9], 71), 0),
        "coupling": gaussian(key_of[7], (FS, N_FRONT * CR), FS ** -0.5, 0.0625, ((0, 8), (1, 4))),
        "front_sizes": place_ends(jax.random.randint(key_of[8], (FRONTS,), FS // 2, FS + 1), jax.random.fold_in(key_of[8], 1), FS // 2, FS).astype(jnp.int32),
    }


def level_shape(level_at):
    share_count = N_FRONT >> (LEVELS - 1 - level_at)
    return share_count, FS // share_count


def level_offset(level_at):
    return sum(level_shape(other)[1] for other in range(level_at))


def take_level(matrix, level_at):
    share_count, block_rows = level_shape(level_at)
    offset = level_offset(level_at)
    sliced = matrix.reshape(N_FRONT, LR, matrix.shape[-1])[:, offset:offset + block_rows]
    return sliced.reshape(N_FRONT // share_count, FS, matrix.shape[-1])


def couple_level(coupling, level_at):
    share_count, block_rows = level_shape(level_at)
    offset = level_offset(level_at)
    sliced = coupling.reshape(FS, N_FRONT, CR)[:, :, offset:offset + block_rows]
    return sliced.reshape(FS, N_FRONT // share_count, FS).transpose(1, 0, 2)


def level_mask(front_sizes, level_at):
    front_count = 2 ** (LEVELS - 1 - level_at)
    first_front = sum(2 ** (LEVELS - 1 - other) for other in range(level_at))
    live_sizes = front_sizes[first_front:first_front + front_count]
    rows_at = jnp.arange(FS, dtype=jnp.int32)
    return (rows_at[None, :, None] < live_sizes[:, None, None]).astype(jnp.float32)


def reference(elem_mat, elem_deriv, elem_disp, elem_sens, design_var, dof_rows, inverse_factor, coupling, front_sizes):
    def add_block(totals, block_index):
        start_row = block_index * E_DEV
        tables = lax.dynamic_slice_in_dim(elem_mat, start_row, E_DEV, 2).astype(jnp.float32)
        derivs = lax.dynamic_slice_in_dim(elem_deriv, start_row, E_DEV, 2).astype(jnp.float32)
        disps = lax.dynamic_slice_in_dim(elem_disp, start_row, E_DEV, 1).astype(jnp.float32)
        sens_block = lax.dynamic_slice_in_dim(elem_sens, start_row, E_DEV, 0).astype(jnp.float32)
        variables = lax.dynamic_slice_in_dim(design_var, start_row, E_DEV, 0)
        places = lax.dynamic_slice_in_dim(dof_rows, start_row, E_DEV, 1).T
        pseudo = -jnp.einsum("ije,ejc->eic", tables, sens_block)
        drive_term = -jnp.einsum("ije,je->ei", derivs, disps)
        hit_column = (jnp.arange(NRHS, dtype=jnp.int32)[None, :] == variables[:, None]).astype(jnp.float32)
        pseudo = pseudo + drive_term[:, :, None] * hit_column[:, None, :]
        front_index = block_index % N_FRONT
        places = jnp.where(places < LR, places + front_index * LR, N_FRONT * LR).astype(jnp.int32)
        totals = totals.at[places.reshape(-1)].add(pseudo.reshape(-1, NRHS), mode="drop")
        return totals, None

    start_loads = jnp.zeros((N_FRONT * LR, NRHS), jnp.float32)
    loads, _ = lax.scan(add_block, start_loads, jnp.arange(ELEMS // E_DEV, dtype=jnp.int32))

    forward_out = []
    acc_rows = None
    for level_at in range(LEVELS):
        live_rows = level_mask(front_sizes, level_at)
        factor_rows = take_level(inverse_factor, level_at).astype(jnp.float32)
        given = take_level(loads, level_at)
        if acc_rows is not None:
            given = given - acc_rows
        rhs_in = (live_rows * given).astype(jnp.bfloat16)
        solved = live_rows * jnp.einsum("nij,njc->nic", factor_rows, rhs_in.astype(jnp.float32))
        forward_out.append(solved)
        if level_at < LEVELS - 1:
            links = couple_level(coupling, level_at).astype(jnp.float32)
            rounded = solved.astype(jnp.bfloat16).astype(jnp.float32)
            partial_value = jnp.einsum("nij,njc->nic", links, rounded)
            acc_rows = partial_value.reshape(partial_value.shape[0] // 2, 2, FS, NRHS).sum(axis=1)

    pieces_out = [None] * LEVELS
    parent_rows = None
    for level_at in reversed(range(LEVELS)):
        live_rows = level_mask(front_sizes, level_at)
        factor_rows = take_level(inverse_factor, level_at).astype(jnp.float32)
        residual = forward_out[level_at]
        if parent_rows is not None:
            links = couple_level(coupling, level_at).astype(jnp.float32)
            spread_parent = jnp.repeat(parent_rows.astype(jnp.float32), 2, axis=0)
            residual = residual - jnp.einsum("nji,njc->nic", links, spread_parent)
        back_in = (live_rows * residual).astype(jnp.bfloat16)
        answer = live_rows * jnp.einsum("nji,njc->nic", factor_rows, back_in.astype(jnp.float32))
        pieces_out[level_at] = answer
        parent_rows = answer.astype(jnp.bfloat16)

    laid_out = [pieces_out[level_at].reshape(N_FRONT, level_shape(level_at)[1], NRHS) for level_at in range(LEVELS)]
    return jnp.concatenate(laid_out, axis=1).reshape(N_FRONT * LR, NRHS)
```

```python
import jax
import jax.numpy as jnp
from jax import lax
from jax.sharding import PartitionSpec as P

FS = 8192
LEVELS = 3
CHUNKS = 2


def swapped(array, axis, bit):
    return lax.ppermute(array, axis, [(i, i ^ 1 << bit) for i in range(lax.axis_size(axis))])


def local_pseudo(tables, derivs, disps, sens, variables):
    column_count = sens.shape[2]
    pseudo = -jnp.einsum("ije,ejc->eic", tables, sens, preferred_element_type=jnp.float32)
    drive_term = -jnp.einsum("ije,je->ei", derivs, disps, preferred_element_type=jnp.float32)
    column_ids = lax.iota(jnp.int32, column_count)
    hit_column = (column_ids[None, :] == variables[:, None]).astype(jnp.float32)
    return pseudo + drive_term[:, :, None] * hit_column[:, None, :]


def scatter_rows(pseudo, places, spot_rows):
    column_count = pseudo.shape[-1]
    term_rows = jnp.zeros((spot_rows, column_count), jnp.float32)
    return term_rows.at[places.T.reshape(-1)].add(
        pseudo.reshape(-1, column_count).astype(jnp.float32), mode="drop"
    )


def sum_group(value, bits):
    for bit_at in bits:
        value = value + swapped(value.astype(jnp.bfloat16), "front", bit_at).astype(jnp.float32)
    return value


def body(
    elem_mat,
    elem_deriv,
    elem_disp,
    elem_sens,
    design_var,
    dof_rows,
    inverse_factor,
    coupling,
    front_sizes,
):
    bf16, f32 = jnp.bfloat16, jnp.float32
    depth_bits = lax.axis_size("front").bit_length() - 1
    elem_count = lax.axis_size("elem")
    device = lax.axis_index("front")
    elem_at = lax.axis_index("elem")
    inner = FS // elem_count
    spot_rows = inverse_factor.shape[0]

    pseudo = local_pseudo(elem_mat, elem_deriv, elem_disp, elem_sens, design_var).astype(bf16)
    places = lax.all_gather(dof_rows, "elem", axis=1, tiled=True)
    own_pseudo = lax.all_to_all(pseudo, "elem", split_axis=2, concat_axis=0, tiled=True)
    load_rows = scatter_rows(own_pseudo, places, spot_rows).astype(bf16)

    facts = []
    offset = 0
    first_front = 0
    for level_at in range(LEVELS):
        bit_count = depth_bits - (LEVELS - 1 - level_at)
        block_rows = FS >> bit_count
        front_id = first_front + (device >> bit_count)
        size_now = lax.dynamic_index_in_dim(front_sizes, front_id, 0, keepdims=False)
        start = (device & (1 << bit_count) - 1) * block_rows
        shard = block_rows // elem_count
        own_at = start + elem_at * shard + lax.iota(jnp.int32, shard)
        inner_at = elem_at * inner + lax.iota(jnp.int32, inner)
        own_live = (own_at < size_now).astype(f32)[:, None]
        inner_live = (inner_at < size_now).astype(f32)[:, None]
        facts.append((bit_count, block_rows, offset, start, own_live, inner_live))
        offset = offset + block_rows
        first_front = first_front + (1 << LEVELS - 1 - level_at)

    given = []
    for level_at in range(LEVELS):
        bit_count, block_rows, offset, start, own_live, inner_live = facts[level_at]
        piece = load_rows[offset : offset + block_rows]
        if block_rows < FS:
            spread = jnp.zeros((FS, piece.shape[1]), bf16)
            piece = lax.dynamic_update_slice_in_dim(spread, piece, start, 0)
        given.append(lax.all_to_all(piece, "elem", split_axis=0, concat_axis=1, tiled=True))

    width = given[0].shape[1] // CHUNKS

    def bits_of(bit_count, chunk):
        bits = list(range(bit_count))
        return bits if chunk % 2 == 0 else bits[::-1]

    def scatter_sum(partial_value):
        return lax.psum_scatter(
            partial_value.astype(bf16), "elem", scatter_dimension=0, tiled=True
        ).astype(f32)

    def widen(value):
        return lax.all_gather(value.astype(bf16), "elem", axis=0, tiled=True)

    forward_out = [[None] * CHUNKS for _ in range(LEVELS)]
    wide_out = [None] * CHUNKS
    part = [given[0][:, c * width : (c + 1) * width].astype(f32) for c in range(CHUNKS)]
    for level_at in range(LEVELS):
        bit_count, block_rows, offset, start, own_live, inner_live = facts[level_at]
        factor_rows = inverse_factor[offset : offset + block_rows]
        for c in range(CHUNKS):
            rhs = (inner_live * sum_group(part[c], bits_of(bit_count, c))).astype(bf16)
            solved = own_live * scatter_sum(jnp.dot(factor_rows, rhs, preferred_element_type=f32))
            forward_out[level_at][c] = solved
            wide_out[c] = widen(solved)
            if level_at < LEVELS - 1:
                links = coupling[:, offset : offset + block_rows]
                acc = jnp.dot(links, wide_out[c], preferred_element_type=f32)
                part[c] = given[level_at + 1][:, c * width : (c + 1) * width].astype(f32) - acc

    pieces_out = [None] * LEVELS
    parent = [None] * CHUNKS
    for level_at in reversed(range(LEVELS)):
        bit_count, block_rows, offset, start, own_live, inner_live = facts[level_at]
        factor_rows = inverse_factor[offset : offset + block_rows]
        links = coupling[:, offset : offset + block_rows] if level_at < LEVELS - 1 else None
        for c in range(CHUNKS):
            if level_at == LEVELS - 1:
                wide_back = wide_out[c]
            else:
                correction = lax.dot_general(
                    links, parent[c], (((0,), (0,)), ((), ())), preferred_element_type=f32
                )
                residual = forward_out[level_at][c] - scatter_sum(correction)
                wide_back = widen(own_live * residual)
            partial_value = lax.dot_general(
                factor_rows, wide_back, (((0,), (0,)), ((), ())), preferred_element_type=f32
            )
            answer = inner_live * sum_group(partial_value, bits_of(bit_count, c))
            parent[c] = answer.astype(bf16)
        whole = jnp.concatenate(parent, 1)
        turned = lax.all_to_all(whole, "elem", split_axis=1, concat_axis=0, tiled=True)
        pieces_out[level_at] = lax.dynamic_slice_in_dim(turned, start, block_rows, 0)
    return jnp.concatenate(pieces_out, 0).astype(f32)


def solution(mesh):
    return jax.shard_map(
        body,
        mesh=mesh,
        in_specs=(
            P(None, None, ("elem", "front")),
            P(None, None, ("elem", "front")),
            P(None, ("elem", "front")),
            P(("elem", "front"), None, None),
            P(("elem", "front")),
            P(None, ("elem", "front")),
            P("front", "elem"),
            P("elem", "front"),
            P(),
        ),
        out_specs=P("front", "elem"),
        check_vma=False,
    )
```

```python
import jax
import jax.numpy as jnp
from jax import lax
from jax.experimental import pallas as pl
from jax.experimental.pallas import tpu as pltpu
from jax.sharding import PartitionSpec as P

FS = 8192
LEVELS = 3
CHUNKS = 2
BLK = 128
GROUP = 8


def swapped(array, axis, bit):
    return lax.ppermute(array, axis, [(i, i ^ 1 << bit) for i in range(lax.axis_size(axis))])


def local_pseudo(tables, derivs, disps, sens, variables):
    column_count = sens.shape[2]
    pseudo = -jnp.einsum("ije,ejc->eic", tables, sens, preferred_element_type=jnp.float32)
    drive_term = -jnp.einsum("ije,je->ei", derivs, disps, preferred_element_type=jnp.float32)
    column_ids = lax.iota(jnp.int32, column_count)
    hit_column = (column_ids[None, :] == variables[:, None]).astype(jnp.float32)
    return pseudo + drive_term[:, :, None] * hit_column[:, None, :]


def scatter_kernel(blocks_ref, rows_ref, pseudo_ref, out_ref):
    out_ref[...] = jnp.zeros_like(out_ref)
    dof = rows_ref.shape[1]

    def step(group_at, carry):
        first = pl.multiple_of(group_at * GROUP, GROUP)
        rows = rows_ref[pl.ds(first, GROUP), :]
        spread = []
        for at in range(GROUP):
            lanes = jnp.broadcast_to(rows[at : at + 1, :], (BLK, dof))
            hits = lax.broadcasted_iota(jnp.int32, (BLK, dof), 0) == lanes
            spread.append(
                jnp.dot(
                    hits.astype(jnp.float32).astype(jnp.bfloat16),
                    pseudo_ref[first + at],
                    preferred_element_type=jnp.float32,
                )
            )
        for at in range(GROUP):
            block = blocks_ref[first + at]
            out_ref[block] = out_ref[block] + spread[at]
        return carry

    lax.fori_loop(0, rows_ref.shape[0] // GROUP, step, 0)


def scatter_rows(pseudo, places, spot_rows):
    element_count, dof, column_count = pseudo.shape
    block_count = spot_rows // BLK
    places = places.T
    used = places < spot_rows
    blocks = jnp.min(jnp.where(used, places, spot_rows), 1) // BLK
    blocks = jnp.clip(blocks, 0, block_count - 1)
    rows = jnp.where(used, places - blocks[:, None] * BLK, -1)
    spread = pl.pallas_call(
        scatter_kernel,
        out_shape=jax.ShapeDtypeStruct((block_count, BLK, column_count), jnp.float32),
        in_specs=[
            pl.BlockSpec(memory_space=pltpu.SMEM),
            pl.BlockSpec(memory_space=pltpu.VMEM),
            pl.BlockSpec(memory_space=pltpu.VMEM),
        ],
        out_specs=pl.BlockSpec(memory_space=pltpu.VMEM),
        compiler_params=pltpu.CompilerParams(vmem_limit_bytes=40 * 1024 * 1024),
    )(blocks, rows, pseudo)
    return spread.reshape(spot_rows, column_count)


def sum_group(value, bits):
    for bit_at in bits:
        value = value + swapped(value.astype(jnp.bfloat16), "front", bit_at).astype(jnp.float32)
    return value


def body(
    elem_mat,
    elem_deriv,
    elem_disp,
    elem_sens,
    design_var,
    dof_rows,
    inverse_factor,
    coupling,
    front_sizes,
):
    bf16, f32 = jnp.bfloat16, jnp.float32
    depth_bits = lax.axis_size("front").bit_length() - 1
    elem_count = lax.axis_size("elem")
    device = lax.axis_index("front")
    elem_at = lax.axis_index("elem")
    inner = FS // elem_count
    spot_rows = inverse_factor.shape[0]

    pseudo = local_pseudo(elem_mat, elem_deriv, elem_disp, elem_sens, design_var).astype(bf16)
    places = lax.all_gather(dof_rows, "elem", axis=1, tiled=True)
    own_pseudo = lax.all_to_all(pseudo, "elem", split_axis=2, concat_axis=0, tiled=True)
    load_rows = scatter_rows(own_pseudo, places, spot_rows).astype(bf16)

    facts = []
    offset = 0
    first_front = 0
    for level_at in range(LEVELS):
        bit_count = depth_bits - (LEVELS - 1 - level_at)
        block_rows = FS >> bit_count
        front_id = first_front + (device >> bit_count)
        size_now = lax.dynamic_index_in_dim(front_sizes, front_id, 0, keepdims=False)
        start = (device & (1 << bit_count) - 1) * block_rows
        shard = block_rows // elem_count
        own_at = start + elem_at * shard + lax.iota(jnp.int32, shard)
        inner_at = elem_at * inner + lax.iota(jnp.int32, inner)
        own_live = (own_at < size_now).astype(f32)[:, None]
        inner_live = (inner_at < size_now).astype(f32)[:, None]
        facts.append((bit_count, block_rows, offset, start, own_live, inner_live))
        offset = offset + block_rows
        first_front = first_front + (1 << LEVELS - 1 - level_at)

    given = []
    for level_at in range(LEVELS):
        bit_count, block_rows, offset, start, own_live, inner_live = facts[level_at]
        piece = load_rows[offset : offset + block_rows]
        if block_rows < FS:
            spread = jnp.zeros((FS, piece.shape[1]), bf16)
            piece = lax.dynamic_update_slice_in_dim(spread, piece, start, 0)
        given.append(lax.all_to_all(piece, "elem", split_axis=0, concat_axis=1, tiled=True))

    width = given[0].shape[1] // CHUNKS

    def bits_of(bit_count, chunk):
        bits = list(range(bit_count))
        return bits if chunk % 2 == 0 else bits[::-1]

    def scatter_sum(partial_value):
        return lax.psum_scatter(partial_value, "elem", scatter_dimension=0, tiled=True)

    def widen(value):
        return lax.all_gather(value, "elem", axis=0, tiled=True)

    last = []

    def in_turn(chunk, operand, transfer, results):
        if last:
            held, at = last.pop()
            held[at], operand = lax.optimization_barrier((held[at], operand))
        results[chunk] = transfer(operand)
        last.append((results, chunk))

    chunks = range(CHUNKS)
    forward_out = []
    part = [given[0][:, c * width : (c + 1) * width].astype(f32) for c in chunks]
    for level_at in range(LEVELS):
        bit_count, block_rows, offset, start, own_live, inner_live = facts[level_at]
        factor_rows = inverse_factor[offset : offset + block_rows]
        sums, wide = [None] * CHUNKS, [None] * CHUNKS
        for c in chunks:
            if level_at:
                links = coupling[:, links_at : links_at + links_rows]
                acc = jnp.dot(links, wide_before[c], preferred_element_type=f32)
                part[c] = given[level_at][:, c * width : (c + 1) * width].astype(f32) - acc
            rhs = (inner_live * sum_group(part[c], bits_of(bit_count, c))).astype(bf16)
            product = jnp.dot(factor_rows, rhs, preferred_element_type=f32).astype(bf16)
            in_turn(c, product, scatter_sum, sums)
        for c in chunks:
            in_turn(c, (own_live * sums[c].astype(f32)).astype(bf16), widen, wide)
        forward_out.append([own_live * sums[c].astype(f32) for c in chunks])
        wide_before, links_at, links_rows = wide, offset, block_rows

    pieces_out = [None] * LEVELS
    answers = [None] * CHUNKS
    for level_at in reversed(range(LEVELS)):
        bit_count, block_rows, offset, start, own_live, inner_live = facts[level_at]
        factor_rows = inverse_factor[offset : offset + block_rows]
        if level_at == LEVELS - 1:
            wide = wide_before
        else:
            links = coupling[:, offset : offset + block_rows]
            sums, next_wide = [None] * CHUNKS, [None] * CHUNKS
            for c in chunks:
                answers[c] = answer_of(c, upper, wide)
                correction = lax.dot_general(
                    links, answers[c], (((0,), (0,)), ((), ())), preferred_element_type=f32
                ).astype(bf16)
                in_turn(c, correction, scatter_sum, sums)
            pieces_out[level_at + 1] = piece_of(answers, upper)
            for c in chunks:
                residual = forward_out[level_at][c] - sums[c].astype(f32)
                in_turn(c, (own_live * residual).astype(bf16), widen, next_wide)
            wide = next_wide

        def answer_of(chunk, facts_at, wide_rows):
            rows, live, bits = facts_at[:3]
            partial_value = lax.dot_general(
                rows, wide_rows[chunk], (((0,), (0,)), ((), ())), preferred_element_type=f32
            )
            return (live * sum_group(partial_value, bits_of(bits, chunk))).astype(bf16)

        def piece_of(parts, facts_at):
            whole = jnp.concatenate(parts, 1)
            turned = lax.all_to_all(whole, "elem", split_axis=1, concat_axis=0, tiled=True)
            return lax.dynamic_slice_in_dim(turned, facts_at[3], facts_at[4], 0)

        upper = (factor_rows, inner_live, bit_count, start, block_rows)
    answers = [answer_of(c, upper, wide) for c in chunks]
    pieces_out[0] = piece_of(answers, upper)
    return jnp.concatenate(pieces_out, 0).astype(f32)


def solution(mesh):
    return jax.shard_map(
        body,
        mesh=mesh,
        in_specs=(
            P(None, None, ("elem", "front")),
            P(None, None, ("elem", "front")),
            P(None, ("elem", "front")),
            P(("elem", "front"), None, None),
            P(("elem", "front")),
            P(None, ("elem", "front")),
            P("front", "elem"),
            P("elem", "front"),
            P(),
        ),
        out_specs=P("front", "elem"),
        check_vma=False,
    )
```

```python
import jax
import jax.numpy as jnp
from jax import lax
from jax.experimental import pallas as pl
from jax.experimental.pallas import tpu as pltpu
from jax.sharding import PartitionSpec as P

FS = 8192
LEVELS = 3
CHUNKS = 2
BLK = 128
GROUP = 8


def swapped(array, axis, bit):
    return lax.ppermute(array, axis, [(i, i ^ 1 << bit) for i in range(lax.axis_size(axis))])


def local_pseudo(tables, derivs, disps, sens, variables):
    column_count = sens.shape[2]
    pseudo = -jnp.einsum("ije,ejc->eic", tables, sens, preferred_element_type=jnp.float32)
    drive_term = -jnp.einsum("ije,je->ei", derivs, disps, preferred_element_type=jnp.float32)
    column_ids = lax.iota(jnp.int32, column_count)
    hit_column = (column_ids[None, :] == variables[:, None]).astype(jnp.float32)
    return pseudo + drive_term[:, :, None] * hit_column[:, None, :]


def scatter_kernel(blocks_ref, rows_ref, pseudo_ref, out_ref):
    out_ref[...] = jnp.zeros_like(out_ref)
    dof = rows_ref.shape[1]

    def step(group_at, carry):
        first = pl.multiple_of(group_at * GROUP, GROUP)
        rows = rows_ref[pl.ds(first, GROUP), :]
        spread = []
        for at in range(GROUP):
            lanes = jnp.broadcast_to(rows[at : at + 1, :], (BLK, dof))
            hits = lax.broadcasted_iota(jnp.int32, (BLK, dof), 0) == lanes
            spread.append(
                jnp.dot(
                    hits.astype(jnp.float32).astype(jnp.bfloat16),
                    pseudo_ref[first + at],
                    preferred_element_type=jnp.float32,
                )
            )
        for at in range(GROUP):
            block = blocks_ref[first + at]
            out_ref[block] = out_ref[block] + spread[at]
        return carry

    lax.fori_loop(0, rows_ref.shape[0] // GROUP, step, 0)


def scatter_rows(pseudo, places, spot_rows):
    element_count, dof, column_count = pseudo.shape
    block_count = spot_rows // BLK
    places = places.T
    used = places < spot_rows
    blocks = jnp.min(jnp.where(used, places, spot_rows), 1) // BLK
    blocks = jnp.clip(blocks, 0, block_count - 1)
    rows = jnp.where(used, places - blocks[:, None] * BLK, -1)
    spread = pl.pallas_call(
        scatter_kernel,
        out_shape=jax.ShapeDtypeStruct((block_count, BLK, column_count), jnp.float32),
        in_specs=[
            pl.BlockSpec(memory_space=pltpu.SMEM),
            pl.BlockSpec(memory_space=pltpu.VMEM),
            pl.BlockSpec(memory_space=pltpu.VMEM),
        ],
        out_specs=pl.BlockSpec(memory_space=pltpu.VMEM),
        compiler_params=pltpu.CompilerParams(vmem_limit_bytes=40 * 1024 * 1024),
    )(blocks, rows, pseudo)
    return spread.reshape(spot_rows, column_count)


def sum_group(value, bits):
    for bit_at in bits:
        value = value + swapped(value.astype(jnp.bfloat16), "front", bit_at).astype(jnp.float32)
    return value


def body(
    elem_mat,
    elem_deriv,
    elem_disp,
    elem_sens,
    design_var,
    dof_rows,
    inverse_factor,
    coupling,
    front_sizes,
):
    bf16, f32 = jnp.bfloat16, jnp.float32
    depth_bits = lax.axis_size("front").bit_length() - 1
    elem_count = lax.axis_size("elem")
    device = lax.axis_index("front")
    elem_at = lax.axis_index("elem")
    inner = FS // elem_count
    spot_rows = inverse_factor.shape[0]

    pseudo = local_pseudo(elem_mat, elem_deriv, elem_disp, elem_sens, design_var).astype(bf16)
    places = lax.all_gather(dof_rows, "elem", axis=1, tiled=True)
    own_pseudo = lax.all_to_all(pseudo, "elem", split_axis=2, concat_axis=0, tiled=True)
    load_rows = scatter_rows(own_pseudo, places, spot_rows).astype(bf16)

    facts = []
    offset = 0
    first_front = 0
    for level_at in range(LEVELS):
        bit_count = depth_bits - (LEVELS - 1 - level_at)
        block_rows = FS >> bit_count
        front_id = first_front + (device >> bit_count)
        size_now = lax.dynamic_index_in_dim(front_sizes, front_id, 0, keepdims=False)
        start = (device & (1 << bit_count) - 1) * block_rows
        shard = block_rows // elem_count
        own_at = start + elem_at * shard + lax.iota(jnp.int32, shard)
        inner_at = elem_at * inner + lax.iota(jnp.int32, inner)
        own_live = (own_at < size_now).astype(f32)[:, None]
        inner_live = (inner_at < size_now).astype(f32)[:, None]
        facts.append((bit_count, block_rows, offset, start, own_live, inner_live))
        offset = offset + block_rows
        first_front = first_front + (1 << LEVELS - 1 - level_at)

    def in_group(value, share):
        count = lax.axis_size("front")
        groups = [list(range(i, i + share)) for i in range(0, count, share)]
        return lax.all_to_all(
            value, "front", split_axis=0, concat_axis=0, tiled=True, axis_index_groups=groups
        )

    given = []
    for level_at in range(LEVELS):
        bit_count, block_rows, offset, start, own_live, inner_live = facts[level_at]
        piece = load_rows[offset : offset + block_rows]
        share = 1 << bit_count
        if share > 1:
            piece = piece.reshape(elem_count // share, share, inner // share, -1)
            piece = in_group(piece.swapaxes(0, 1), share).reshape(elem_count * (inner // share), -1)
        turned = lax.all_to_all(piece, "elem", split_axis=0, concat_axis=1, tiled=True)
        if share > 1:
            at = (device & share - 1) * (inner // share)
            zeros = jnp.zeros((inner, turned.shape[1]), bf16)
            turned = lax.dynamic_update_slice_in_dim(zeros, turned, at, 0)
        given.append(turned)

    width = given[0].shape[1] // CHUNKS

    def bits_of(bit_count, chunk):
        bits = list(range(bit_count))
        return bits if chunk % 2 == 0 else bits[::-1]

    def scatter_sum(partial_value):
        return lax.psum_scatter(partial_value, "elem", scatter_dimension=0, tiled=True)

    def widen(value):
        return lax.all_gather(value, "elem", axis=0, tiled=True)

    last = []

    def in_turn(chunk, operand, transfer, results):
        if last:
            held, at = last.pop()
            held[at], operand = lax.optimization_barrier((held[at], operand))
        results[chunk] = transfer(operand)
        last.append((results, chunk))

    chunks = range(CHUNKS)
    forward_out = []
    part = [given[0][:, c * width : (c + 1) * width].astype(f32) for c in chunks]
    for level_at in range(LEVELS):
        bit_count, block_rows, offset, start, own_live, inner_live = facts[level_at]
        factor_rows = inverse_factor[offset : offset + block_rows]
        sums, wide = [None] * CHUNKS, [None] * CHUNKS
        for c in chunks:
            if level_at:
                links = coupling[:, links_at : links_at + links_rows]
                acc = jnp.dot(links, wide_before[c], preferred_element_type=f32)
                part[c] = given[level_at][:, c * width : (c + 1) * width].astype(f32) - acc
            rhs = (inner_live * sum_group(part[c], bits_of(bit_count, c))).astype(bf16)
            product = jnp.dot(factor_rows, rhs, preferred_element_type=f32).astype(bf16)
            in_turn(c, product, scatter_sum, sums)
        for c in chunks:
            in_turn(c, (own_live * sums[c].astype(f32)).astype(bf16), widen, wide)
        forward_out.append([own_live * sums[c].astype(f32) for c in chunks])
        wide_before, links_at, links_rows = wide, offset, block_rows

    pieces_out = [None] * LEVELS
    answers = [None] * CHUNKS
    for level_at in reversed(range(LEVELS)):
        bit_count, block_rows, offset, start, own_live, inner_live = facts[level_at]
        factor_rows = inverse_factor[offset : offset + block_rows]
        if level_at == LEVELS - 1:
            wide = wide_before
        else:
            links = coupling[:, offset : offset + block_rows]
            sums, next_wide = [None] * CHUNKS, [None] * CHUNKS
            for c in chunks:
                answers[c] = answer_of(c, upper, wide)
                correction = lax.dot_general(
                    links, answers[c], (((0,), (0,)), ((), ())), preferred_element_type=f32
                ).astype(bf16)
                in_turn(c, correction, scatter_sum, sums)
            pieces_out[level_at + 1] = piece_of(answers, upper)
            for c in chunks:
                residual = forward_out[level_at][c] - sums[c].astype(f32)
                in_turn(c, (own_live * residual).astype(bf16), widen, next_wide)
            wide = next_wide

        def answer_of(chunk, facts_at, wide_rows):
            rows, live, bits = facts_at[:3]
            partial_value = lax.dot_general(
                rows, wide_rows[chunk], (((0,), (0,)), ((), ())), preferred_element_type=f32
            )
            return (live * sum_group(partial_value, bits_of(bits, chunk))).astype(bf16)

        def piece_of(parts, facts_at):
            whole = jnp.concatenate(parts, 1)
            share = 1 << facts_at[2]
            if share > 1:
                at = (device & share - 1) * (inner // share)
                whole = lax.dynamic_slice_in_dim(whole, at, inner // share, 0)
            turned = lax.all_to_all(whole, "elem", split_axis=1, concat_axis=0, tiled=True)
            if share > 1:
                turned = turned.reshape(share, elem_count // share, inner // share, -1)
                turned = in_group(turned, share).swapaxes(0, 1).reshape(facts_at[4], -1)
            return turned

        upper = (factor_rows, inner_live, bit_count, start, block_rows)
    answers = [answer_of(c, upper, wide) for c in chunks]
    pieces_out[0] = piece_of(answers, upper)
    return jnp.concatenate(pieces_out, 0).astype(f32)


def solution(mesh):
    return jax.shard_map(
        body,
        mesh=mesh,
        in_specs=(
            P(None, None, ("elem", "front")),
            P(None, None, ("elem", "front")),
            P(None, ("elem", "front")),
            P(("elem", "front"), None, None),
            P(("elem", "front")),
            P(None, ("elem", "front")),
            P("front", "elem"),
            P("elem", "front"),
            P(),
        ),
        out_specs=P("front", "elem"),
        check_vma=False,
    )
```
